32 devices in a mesh: owner: 4 (over z), rows: 8 (over y, x, core).
Axes of the slice: x: 2, y: 2, z: 4, core: 2. Of those that a mesh axis runs over, the one named last changes fastest.
Arguments:
- w_gate: float32 [128, 2048, 768], P('owner', 'rows'), may hold values from -0.1875 to 0.1875
- w_up: float32 [128, 2048, 768], P('owner', 'rows'), may hold values from -0.1875 to 0.1875
- router_weight: float32 [2048, 128], P('rows', 'owner'), may hold values from -0.125 to 0.125
- router_gain: float32 [2048], P('rows'), may hold values from 0.25 to 1.75
Outputs:
- serve_gate: bfloat16 [128, 2048, 768], P('owner', None, 'rows')
- serve_up: bfloat16 [128, 2048, 768], P('owner', None, 'rows')
- scale_gate: float32 [128, 768], P('owner', 'rows')
- scale_up: float32 [128, 768], P('owner', 'rows')
- serve_router: bfloat16 [2048, 128], replicated
The draws below stay inside these ranges and needn't reach their ends.
All inputs are finite; a program needn't handle non-finite values. Where the reference program divides by a largest or mean magnitude, that divisor is 1e-20 or more.
Results may differ from the reference program's by a relative error of at most 0.001.
Values may be sent and summed in bfloat16 or wider, within the bound.
A program may use at most 192 MiB of HBM per device.

```python
import jax
import jax.numpy as jnp

EXPERTS = 128
D_MODEL = 2048
D_EXPERT = 768


def spiked(result, key, source, target, blocks, factor):
    owner, partner = [(jnp.arange(result.shape[dim]) // (result.shape[dim] // blocks)).reshape([-1 if axis == dim else 1 for axis in range(result.ndim)]) for dim in (source, target)]
    chosen = jax.random.permutation(key, blocks)[partner]
    strong = (owner == chosen) | (owner == (partner + blocks // 2) % blocks)
    return jnp.where(strong, factor * result, result)


def shard_levels(stream_key, extent, cuts, least, high):
    factor_of = 1.0
    for axis_at, parts in cuts:
        draws = jax.random.uniform(jax.random.fold_in(jax.random.fold_in(stream_key, 6), axis_at), (parts,), jnp.float32, least / len(cuts), high / len(cuts))
        factor_of = factor_of * jnp.repeat(jnp.exp(draws), extent[axis_at] // parts).reshape((-1,) + (1,) * (len(extent) - 1 - axis_at))
    return factor_of


def bell_draw(key, extent, spread, reach, cuts=(), held_as=jnp.bfloat16):
    loudness = shard_levels(key, extent, cuts, -0.22, 0.18) if cuts else 1.0
    entries = jax.random.normal(key, extent, jnp.float32) * spread * loudness
    return jnp.minimum(jnp.maximum(entries, -reach), reach).astype(held_as)


def bell_draw_with(key, dims, deviation, most, pieces, heavy, held_as=jnp.bfloat16):
    drawn = deviation * jax.random.normal(key, dims, jnp.float32)
    if pieces:
        drawn = drawn * shard_levels(key, dims, pieces, -0.22, 0.18)
    return jnp.clip(spiked(drawn, jax.random.fold_in(key, 3), *heavy), -most, most).astype(held_as)


def setup_inputs(seed: int = 0) -> dict:
    keys = jax.random.split(jax.random.key(seed), 5)
    w_gate = bell_draw_with(keys[0], (EXPERTS, D_MODEL, D_EXPERT), D_MODEL ** -0.5, 0.1875, ((0, 4), (1, 8)), (1, 2, 8, 2.0), jnp.float32)
    w_up = bell_draw_with(keys[1], (EXPERTS, D_MODEL, D_EXPERT), D_MODEL ** -0.5, 0.1875, ((0, 4), (1, 8)), (1, 2, 8, 2.0), jnp.float32)
    router_weight = bell_draw(keys[2], (D_MODEL, EXPERTS), D_MODEL ** -0.5, 0.125, ((0, 8), (1, 4)), jnp.float32)
    router_gain = jnp.clip(1.0 + 0.15 * jax.random.normal(keys[3], (D_MODEL,), jnp.float32), 0.25, 1.75)
    return {"w_gate": w_gate, "w_up": w_up, "router_weight": router_weight, "router_gain": router_gain}


def reference(w_gate, w_up, router_weight, router_gain):
    scale_gate = jnp.sum(jnp.abs(w_gate), axis=1) / D_MODEL
    serve_gate = (w_gate / jnp.expand_dims(scale_gate, 1)).astype(jnp.bfloat16)
    scale_up = jnp.sum(jnp.abs(w_up), axis=1) / D_MODEL
    serve_up = (w_up / jnp.expand_dims(scale_up, 1)).astype(jnp.bfloat16)
    serve_router = (router_weight * router_gain[:, None]).astype(jnp.bfloat16)
    return serve_gate, serve_up, scale_gate, scale_up, serve_router
```

```python
import functools

import jax
import jax.numpy as jnp
from jax import lax
from jax.experimental import pallas as pl
from jax.experimental.pallas import tpu as pltpu
from jax.sharding import PartitionSpec as P

MESH = pl.DeviceIdType.MESH
WINDOW = 6
LOADS = 3
PAIR_LAG = 2
LAG = 4
HELD = LOADS + LAG
SUMS = 2 * LAG + 2


def peer_steps(n):
    far = list(range(2, n, 2))
    return far + [k + 1 for k in far] + [1]


def toggled(index, k):
    result, bit = index, 1
    while bit <= k:
        if k & bit:
            result = result + bit * (1 - 2 * lax.rem(index // bit, 2))
        bit *= 2
    return result


def exchange(
    experts, n, owners, depth,
    gate, up, router, gain,
    pieces, routed, scales,
    window, stage, row_block, part, partner, both, others,
    load_sem, send_sem, recv_sem, self_sem, pair_send, pair_recv, sum_send, sum_recv,
    own_sem, z_send, z_recv, r_send, r_recv,
):
    me, mine = lax.axis_index("rows"), lax.axis_index("owner")
    units, piece, width = 2 * experts, pieces.shape[2], gate.shape[2]
    peers = [toggled(me, k) for k in peer_steps(n)]
    alike = [toggled(me, k) for k in range(2, n, 2)]
    columns = [lax.rem(mine + k, owners) for k in range(1, owners)]

    barrier = pltpu.get_barrier_semaphore()
    for p in peers:
        pl.semaphore_signal(barrier, inc=1, device_id=(mine, p), device_id_type=MESH)
    for c in columns:
        pl.semaphore_signal(barrier, inc=1, device_id=(c, me), device_id_type=MESH)

    def load(s, go):
        for matrix, first in ((gate, 0), (up, experts)):
            @pl.when((s >= first) & (s < first + experts))
            def _():
                slot = lax.rem(s, HELD)
                copy = pltpu.make_async_copy(matrix.at[s - first], window.at[slot], load_sem.at[slot])
                copy.start() if go else copy.wait()

    def pair(s):
        slot = lax.rem(s, SUMS)
        return pltpu.make_async_remote_copy(
            part.at[s], partner.at[s], pair_send.at[slot], pair_recv.at[slot],
            device_id=(mine, toggled(me, 1)), device_id_type=MESH,
        )

    def chips(s):
        slot = lax.rem(s, SUMS)
        return [
            pltpu.make_async_remote_copy(
                both.at[s], others.at[s, i], sum_send.at[slot, i], sum_recv.at[slot, i],
                device_id=(mine, p), device_id_type=MESH,
            )
            for i, p in enumerate(alike)
        ]

    def parts(s):
        slot, land = lax.rem(s, WINDOW), lax.rem(s, 2 * WINDOW)

        def cut(p):
            return stage.at[slot, pl.ds(pl.multiple_of(p * piece, piece), piece)]

        far = [
            pltpu.make_async_remote_copy(
                cut(p), pieces.at[s, me], send_sem.at[slot, i], recv_sem.at[land, i],
                device_id=(mine, p), device_id_type=MESH,
            )
            for i, p in enumerate(peers)
        ]
        return far, pltpu.make_async_copy(cut(me), pieces.at[s, me], self_sem.at[slot])

    def send(s):
        far, near = parts(s)
        for copy in far:
            copy.start()
        near.start()

    def settle(s):
        far, near = parts(s)
        for copy in far:
            copy.wait()
        near.wait()

    def summed(s):
        part[s] = jnp.sum(jnp.abs(window[lax.rem(s, HELD)]), axis=0, keepdims=True)

    def scaled(s):
        slot, held = lax.rem(s, WINDOW), lax.rem(s, HELD)
        total = both[s]
        for i in range(len(alike)):
            total = total + others[s, i]
        scale = total / depth
        scales[s] = scale
        inverse = 1.0 / scale
        for at in range(0, width, 128):
            w = window[held, :, at : at + 128] * inverse[:, at : at + 128]
            stage[slot, at : at + 128, :] = w.T.astype(jnp.bfloat16)

    row_block[...] = (router[...] * gain[...]).astype(jnp.bfloat16)
    own = pltpu.make_async_copy(row_block, routed.at[me, mine], own_sem)
    along_z = [
        pltpu.make_async_remote_copy(
            row_block, routed.at[me, mine], z_send.at[i], z_recv.at[i],
            device_id=(c, me), device_id_type=MESH,
        )
        for i, c in enumerate(columns)
    ]
    along_rows = [
        pltpu.make_async_remote_copy(
            routed.at[me], routed.at[me], r_send.at[i], r_recv.at[i],
            device_id=(mine, p), device_id_type=MESH,
        )
        for i, p in enumerate(peers)
    ]

    for s in range(LOADS):
        load(jnp.int32(s), True)
    pl.semaphore_wait(barrier, len(peers) + len(columns))

    @pl.loop(0, units + LAG + 1)
    def _(i):
        @pl.when(i < units)
        def _():
            load(i, False)
            summed(i)

        @pl.when((i >= PAIR_LAG) & (i < units + PAIR_LAG))
        def _():
            s = i - PAIR_LAG
            pair(s).wait()
            both[s] = part[s] + partner[s]

        @pl.when((i >= LAG) & (i < units + LAG))
        def _():
            s = i - LAG

            @pl.when(s >= WINDOW)
            def _():
                settle(s - WINDOW)

            for copy in chips(s):
                copy.wait()
            scaled(s)

        @pl.when(i < units)
        def _():
            pair(i).start()

        @pl.when((i >= PAIR_LAG) & (i < units + PAIR_LAG))
        def _():
            for copy in chips(i - PAIR_LAG):
                copy.start()

        load(i + LOADS, True)

        @pl.when(i >= LAG + 1)
        def _():
            send(i - LAG - 1)

        @pl.when(i == LAG + 2)
        def _():
            own.start()
            for copy in along_z:
                copy.start()

        @pl.when(i == units // 2)
        def _():
            own.wait()
            for copy in along_z:
                copy.wait()
            for copy in along_rows:
                copy.start()

    @pl.loop(max(units - WINDOW, 0), units)
    def _(s):
        settle(s)

    for copy in along_rows:
        copy.wait()


def arrange(n, routed, gate_in, up_in, gate_out, up_out, router_out):
    rest = gate_in.shape[3]
    for source, target in ((gate_in, gate_out), (up_in, up_out)):
        for p in range(n):
            target[0, :, p * rest : (p + 1) * rest] = source[0, p]

    @pl.when(pl.program_id(0) == 0)
    def _():
        for p in range(n):
            block = routed[p].astype(jnp.float32).reshape(-1, rest)
            router_out[p * rest : (p + 1) * rest, :] = block.T.astype(jnp.bfloat16)


def in_kernels(n, owners, w_gate, w_up, router_weight, router_gain):
    experts, rows, width = w_gate.shape
    piece, units, across = width // n, 2 * experts, router_weight.shape[1]
    depth = n * rows
    anywhere, vmem = pl.BlockSpec(memory_space=pl.ANY), pl.BlockSpec(memory_space=pltpu.VMEM)
    dma = pltpu.SemaphoreType.DMA
    pieces, routed, scales = pl.pallas_call(
        functools.partial(exchange, experts, n, owners, float(depth)),
        out_shape=(
            jax.ShapeDtypeStruct((units, n, piece, rows), jnp.bfloat16),
            jax.ShapeDtypeStruct((n, owners, across, rows), jnp.bfloat16),
            jax.ShapeDtypeStruct((units, 1, width), jnp.float32),
        ),
        in_specs=[anywhere, anywhere, vmem, vmem],
        out_specs=(anywhere, anywhere, vmem),
        scratch_shapes=[
            pltpu.VMEM((HELD, rows, width), jnp.float32),
            pltpu.VMEM((WINDOW, width, rows), jnp.bfloat16),
            pltpu.VMEM((across, rows), jnp.bfloat16),
            pltpu.VMEM((units, 1, width), jnp.float32),
            pltpu.VMEM((units, 1, width), jnp.float32),
            pltpu.VMEM((units, 1, width), jnp.float32),
            pltpu.VMEM((units, n // 2 - 1, 1, width), jnp.float32),
            dma((HELD,)), dma((WINDOW, n - 1)), dma((2 * WINDOW, n - 1)), dma((WINDOW,)),
            dma((SUMS,)), dma((SUMS,)), dma((SUMS, n // 2 - 1)), dma((SUMS, n // 2 - 1)),
            dma, dma((owners,)), dma((owners,)), dma((n - 1,)), dma((n - 1,)),
        ],
        compiler_params=pltpu.CompilerParams(
            collective_id=0, has_side_effects=True, vmem_limit_bytes=32 * 2**20
        ),
        name="exchange",
    )(w_gate, w_up, router_weight.T, router_gain[None, :])
    own_scale = lax.dynamic_slice_in_dim(
        scales[:, 0, :], lax.axis_index("rows") * piece, piece, axis=1
    )

    full = lambda shape: pl.BlockSpec(shape, lambda e: (0,) * len(shape))
    gate, up, router = pl.pallas_call(
        functools.partial(arrange, n),
        grid=(experts,),
        out_shape=(
            jax.ShapeDtypeStruct((experts, piece, depth), jnp.bfloat16),
            jax.ShapeDtypeStruct((experts, piece, depth), jnp.bfloat16),
            jax.ShapeDtypeStruct((depth, owners * across), jnp.bfloat16),
        ),
        in_specs=[
            full(routed.shape),
            pl.BlockSpec((1, n, piece, rows), lambda e: (e, 0, 0, 0)),
            pl.BlockSpec((1, n, piece, rows), lambda e: (experts + e, 0, 0, 0)),
        ],
        out_specs=(
            pl.BlockSpec((1, piece, depth), lambda e: (e, 0, 0)),
            pl.BlockSpec((1, piece, depth), lambda e: (e, 0, 0)),
            full((depth, owners * across)),
        ),
        compiler_params=pltpu.CompilerParams(
            dimension_semantics=("arbitrary",), vmem_limit_bytes=32 * 2**20
        ),
        name="arrange",
    )(routed, pieces, pieces)
    return (
        jnp.swapaxes(gate, 1, 2), jnp.swapaxes(up, 1, 2),
        own_scale[:experts], own_scale[experts:], router,
    )


def in_ops(n, w_gate, w_up, router_weight, router_gain):
    depth = n * w_gate.shape[1]
    sums = (jnp.sum(jnp.abs(w_gate), axis=1), jnp.sum(jnp.abs(w_up), axis=1))
    served, scales = [], []
    for w, total in zip((w_gate, w_up), lax.psum(sums, "rows")):
        scale = total / depth
        narrow = (w / jnp.expand_dims(scale, 1)).astype(jnp.bfloat16)
        piece = lax.all_to_all(narrow, "rows", split_axis=2, concat_axis=1, tiled=True)
        size = piece.shape[2]
        served.append(piece)
        scales.append(lax.dynamic_slice_in_dim(scale, lax.axis_index("rows") * size, size, axis=1))
    part = (router_weight * router_gain[:, None]).astype(jnp.bfloat16)
    router = lax.all_gather(part, "rows", axis=0, tiled=True)
    router = lax.all_gather(router, "owner", axis=1, tiled=True)
    return (*served, *scales, router)


def solution(mesh):
    n, owners = mesh.shape["rows"], mesh.shape["owner"]

    def on_device(w_gate, w_up, router_weight, router_gain):
        experts, rows, width = w_gate.shape
        whole_tiles = (
            rows % 128 == 0 and width % (16 * n) == 0 and width % 128 == 0
            and n & (n - 1) == 0 and n > 2 and owners > 1
        )
        if whole_tiles:
            return in_kernels(n, owners, w_gate, w_up, router_weight, router_gain)
        return in_ops(n, w_gate, w_up, router_weight, router_gain)

    placed = (P("owner", "rows", None), P("owner", "rows", None), P("rows", "owner"), P("rows"))
    return jax.shard_map(
        on_device,
        mesh=mesh,
        in_specs=placed,
        out_specs=(
            P("owner", None, "rows"),
            P("owner", None, "rows"),
            P("owner", "rows"),
            P("owner", "rows"),
            P(),
        ),
        check_vma=False,
    )
```
